32 devices in a mesh: expert: 16 (over z, y, x), mp: 2 (over core).
Axes of the slice: x: 2, y: 2, z: 4, core: 2. Of those that a mesh axis runs over, the one named last changes fastest.
Arguments:
- tokens: bfloat16 [2048, 2048], P('expert', 'mp'), may hold values from -6 to 6
- expert_ids: int32 [2048, 2], P('expert'), may hold values from 0 to 15, all different within a row; in each aligned block of 128 rows (0 to 127, 128 to 255, ...) at most 32 rows name the same one
- combine: float32 [2048, 2], P('expert'), may hold values from 0.2 to 1
- w_gate: bfloat16 [16, 2048, 2048], P('expert', None, 'mp'), may hold values from -0.125 to 0.125
- w_up: bfloat16 [16, 2048, 2048], P('expert', None, 'mp'), may hold values from -0.125 to 0.125
- w_down: bfloat16 [16, 2048, 2048], P('expert', 'mp'), may hold values from -0.125 to 0.125
- grad_out: bfloat16 [2048, 2048], P('expert', 'mp'), may hold values from -6 to 6
Outputs:
- output: bfloat16 [2048, 2048], P('expert', 'mp')
- grad_tokens: bfloat16 [2048, 2048], P('expert', 'mp')
- grad_down: bfloat16 [16, 2048, 2048], P('expert', 'mp')
The draws below stay inside these ranges and needn't reach their ends.
Inputs may be any that keep to these rules, and one draw needn't show every extreme that they name: `expert_ids`: the ids of a row differ. In each aligned block of 128 rows (the rows of one index of expert) no expert is named by more than 32 rows, and in every draw some block names some expert exactly 32 times.
All inputs are finite; a program needn't handle non-finite values.
Results may differ from the reference program's by a relative error of at most 0.015.
Values may be sent and summed in bfloat16 or wider, within the bound.
No kernel may reach another device: no remote copies, remote signals or barrier semaphores. Data moves between devices by JAX's collectives and lax.ppermute only.
A program may use at most 64 MiB of HBM per device.

```python
import math
import jax
import jax.numpy as jnp
import numpy as np
from jax import lax

D = 2048
FF = 2048
TOP = 2
TOK_DEV = 128
EXPERTS = 16
TOKENS = 2048
HID_DEV = 1024
MOST = 32
N_EXPERT = 16


def block_levels(own_key, dims, cuts, least, top_value):
    def one(dim, parts):
        steps = jax.random.uniform(jax.random.fold_in(jax.random.fold_in(own_key, 6), dim), (parts,), jnp.float32, least / len(cuts), top_value / len(cuts))
        return jnp.repeat(jnp.exp(steps), dims[dim] // parts).reshape((-1,) + (1,) * (len(dims) - dim - 1))

    gain = one(*cuts[0])
    for cut in cuts[1:]:
        gain = gain * one(*cut)
    return gain


def assign_block(stream_key, own, number, rows, number_of, top, most, skew):
    ranking = jax.random.permutation(stream_key, number_of)
    packed, common = portions_of(number_of, rows * top, most, skew, True), portions_of(number_of, rows * top, most, skew, False)
    places = jnp.arange(number_of)

    def named(tallies, rotation):
        used = int((tallies > 0).sum())
        fixed = max(1, used // 4)
        shifted = fixed + (places - fixed + rotation * (used - fixed)) % max(1, number_of - fixed)
        return jnp.zeros((number_of,), jnp.int32).at[ranking[jnp.where(places < fixed, places, shifted)]].set(jnp.asarray(tallies, jnp.int32))

    tallies = jnp.where(number % 4 == 0, named(packed, number // 4), named(common, number - number // 4 - 1))
    mixed = jax.random.permutation(jax.random.fold_in(own, 3), number_of)
    giver, receiver = mixed[0:number_of // 2 * 2:2], mixed[1:number_of // 2 * 2:2]
    slack = jnp.minimum(tallies[giver] - 1, most - tallies[receiver]) // 2
    slack = jnp.where((giver == ranking[0]) | (receiver == ranking[0]) | (tallies[receiver] == 0), 0, jnp.maximum(slack, 0))
    shifted = jax.random.randint(jax.random.fold_in(own, 4), (number_of // 2,), 0, 1 << 20) % (slack + 1)
    tallies = tallies.at[giver].add(-shifted).at[receiver].add(shifted)
    labels = jnp.searchsorted(jnp.cumsum(tallies), jnp.arange(rows * top), side="right").astype(jnp.int32)
    grid = labels.reshape(top, rows).T
    grid = grid[jax.random.permutation(jax.random.fold_in(own, 1), rows)]
    rotation = jax.random.randint(jax.random.fold_in(own, 2), (rows, 1), 0, top)
    return jnp.take_along_axis(grid, (jnp.arange(top)[None, :] + rotation) % top, axis=1)


def portions_of(number_of, total, bound, skew, full):
    weights = [(1 << 20) // math.isqrt(standing ** skew) + 1 for standing in range(1, number_of + 1)]
    largest = bound if full else min(bound, max(-(-total // number_of), total * weights[0] // sum(weights)))
    least = 1 if total - largest >= number_of - 1 else 0
    given, rest = [largest] + [least] * (number_of - 1), total - largest - least * (number_of - 1)
    while rest > 0:
        movable = [i for i in range(1, number_of) if given[i] < largest] or [i for i in range(1, number_of) if given[i] < bound]
        pool, left = sum([weights[i] for i in movable]), rest
        for i in movable:
            addition = min(bound - given[i], max(1, left * weights[i] // pool), rest)
            given[i] = given[i] + addition
            rest = rest - addition
    return np.array(given)


def centred(stream_key, shape, spread, bound, pieces=(), kind=jnp.bfloat16):
    gain = block_levels(stream_key, shape, pieces, -0.22, 0.18) if pieces else 1.0
    entries = jax.random.normal(stream_key, shape, jnp.float32) * spread * gain
    return jnp.minimum(jnp.maximum(entries, -bound), bound).astype(kind)


def setup_inputs(seed: int = 0) -> dict:
    key_list = jax.random.split(jax.random.key(seed), 8)
    tokens = centred(key_list[0], (TOKENS, D), 1.0, 6.0, ((0, 16), (1, 2)))
    expert_ids_keys = jax.random.split(jax.random.fold_in(key_list[1], 1), TOKENS // TOK_DEV)
    expert_ids_turns = jax.random.permutation(jax.random.fold_in(key_list[1], 3), TOKENS // TOK_DEV)
    expert_ids = jax.vmap(lambda own, number: assign_block(jax.random.fold_in(key_list[1], 2), own, number, TOK_DEV, EXPERTS, TOP, MOST, 2))(expert_ids_keys, expert_ids_turns).reshape((TOKENS, TOP))
    combine = jnp.clip(0.2 + 0.8 * jax.random.uniform(key_list[2], (TOKENS, TOP), jnp.float32) ** block_levels(key_list[2], (TOKENS, TOP), ((0, 16),), -0.2, 0.2), 0.2, 1.0)
    w_gate = centred(key_list[3], (EXPERTS, D, FF), D ** -0.5, 0.125, ((0, 16), (2, 2)))
    w_up = centred(key_list[4], (EXPERTS, D, FF), D ** -0.5, 0.125, ((0, 16), (2, 2)))
    w_down = centred(key_list[5], (EXPERTS, FF, D), FF ** -0.5, 0.125, ((0, 16), (1, 2)))
    grad_out = centred(key_list[6], (TOKENS, D), 1.0, 6.0, ((0, 16), (1, 2)))
    return dict(tokens=tokens, expert_ids=expert_ids, combine=combine, w_gate=w_gate, w_up=w_up, w_down=w_down, grad_out=grad_out)


def reference(tokens, expert_ids, combine, w_gate, w_up, w_down, grad_out):
    top_count = expert_ids.shape[1]
    capacity = N_EXPERT * MOST
    groups = FF // HID_DEV
    flat_ids = expert_ids.reshape(-1).astype(jnp.int32)
    flat_weight = combine.reshape(-1).astype(jnp.float32)
    sort_order = jnp.argsort(flat_ids, stable=True).astype(jnp.int32)
    counts = jnp.sum((flat_ids[:, None] == jnp.arange(EXPERTS, dtype=jnp.int32)[None, :]).astype(jnp.int32), axis=0)
    starts = (jnp.cumsum(counts) - counts).astype(jnp.int32)
    padded = jnp.concatenate([sort_order, jnp.zeros((capacity,), jnp.int32)])

    def per_expert(running, inputs):
        out_acc, grad_acc = running
        gate_w, up_w, down_w, first_slot, slot_count = inputs
        picked = lax.dynamic_slice(padded, (first_slot,), (capacity,))
        is_valid = jnp.arange(capacity, dtype=jnp.int32) < slot_count
        row_index = picked // top_count
        weight = jnp.where(is_valid, flat_weight[picked], jnp.float32(0.0))
        chosen = jnp.where(is_valid[:, None], tokens[row_index], jnp.zeros((), tokens.dtype))
        gate_value = jnp.dot(chosen, gate_w, preferred_element_type=jnp.float32)
        up_value = jnp.dot(chosen, up_w, preferred_element_type=jnp.float32)
        sigmoid_gate = jax.nn.sigmoid(gate_value)
        hidden = (gate_value * sigmoid_gate * up_value).astype(jnp.bfloat16)
        group_parts = jnp.einsum("rmf,mfd->rmd", hidden.reshape(capacity, groups, HID_DEV).astype(jnp.float32),
                                 down_w.reshape(groups, HID_DEV, D).astype(jnp.float32))
        group_parts = lax.optimization_barrier(group_parts.astype(jnp.bfloat16)).astype(jnp.float32)
        out_acc = out_acc.at[row_index].add(weight[:, None] * jnp.sum(group_parts, axis=1))
        grad_pick = (weight[:, None] * grad_out[row_index].astype(jnp.float32)).astype(jnp.bfloat16)
        grad_hidden = jnp.dot(grad_pick, down_w.T, preferred_element_type=jnp.float32)
        grad_up = (grad_hidden * gate_value * sigmoid_gate).astype(jnp.bfloat16)
        grad_gate = (grad_hidden * up_value * sigmoid_gate * (1.0 + gate_value * (1.0 - sigmoid_gate))).astype(jnp.bfloat16)
        grad_terms = jnp.einsum("rmf,dmf->rmd", grad_gate.reshape(capacity, groups, HID_DEV).astype(jnp.float32),
                                gate_w.reshape(D, groups, HID_DEV).astype(jnp.float32))
        grad_terms = grad_terms + jnp.einsum("rmf,dmf->rmd", grad_up.reshape(capacity, groups, HID_DEV).astype(jnp.float32),
                                             up_w.reshape(D, groups, HID_DEV).astype(jnp.float32))
        grad_terms = lax.optimization_barrier(grad_terms.astype(jnp.bfloat16)).astype(jnp.float32)
        grad_acc = grad_acc.at[row_index].add(jnp.where(is_valid[:, None], jnp.sum(grad_terms, axis=1), jnp.float32(0.0)))
        down_grad = jnp.dot(hidden.T, grad_pick, preferred_element_type=jnp.float32).astype(jnp.bfloat16)
        return (out_acc, grad_acc), down_grad

    zero_acc = jnp.zeros((TOKENS, D), jnp.float32)
    (out_acc, grad_acc), grad_down = lax.scan(per_expert, (zero_acc, zero_acc),
                                              (w_gate, w_up, w_down, starts, counts))
    return out_acc.astype(jnp.bfloat16), grad_acc.astype(jnp.bfloat16), grad_down
```

```python
import functools

import jax
import jax.numpy as jnp
from jax import lax
from jax.experimental import pallas as pl
from jax.experimental.pallas import tpu as pltpu
from jax.sharding import PartitionSpec as P

F32 = jnp.float32
BF16 = jnp.bfloat16


def ranks(ids, experts):
    top, rows = ids.shape
    names = lax.broadcasted_iota(jnp.int32, (experts, rows), 0)
    named = names == ids[0:1, :]
    for k in range(1, top):
        named = named | (names == ids[k : k + 1, :])
    before = lax.broadcasted_iota(jnp.int32, (rows, rows), 0) < lax.broadcasted_iota(
        jnp.int32, (rows, rows), 1
    )
    rank = jnp.dot(
        named.astype(F32).astype(BF16), before.astype(F32).astype(BF16), preferred_element_type=F32
    )
    return names, named, rank


def route_kernel(ids_ref, weight_ref, rows_ref, grads_ref, out_rows_ref, out_grads_ref, *, most):
    ids = ids_ref[...]
    weight = weight_ref[...]
    top, rows = ids.shape
    slots = out_rows_ref.shape[0]
    experts = slots // most
    names, named, rank = ranks(ids, experts)
    place = jnp.where(named, rank, -1.0)
    scale = jnp.zeros((experts, rows), F32)
    for k in range(top):
        scale = scale + jnp.where(names == ids[k : k + 1, :], weight[k : k + 1, :], 0.0)
    want = lax.broadcasted_iota(jnp.int32, (experts, most, rows), 1).astype(F32)
    hit = want == place[:, None, :]
    select = jnp.where(hit, 1.0, 0.0).reshape(slots, rows)
    scaled = jnp.where(hit, jnp.broadcast_to(scale[:, None, :], hit.shape), 0.0).reshape(slots, rows)
    scale_column = jnp.sum(scaled, axis=1, keepdims=True)
    select = select.astype(BF16)
    out_rows_ref[...] = jnp.dot(select, rows_ref[...], preferred_element_type=F32).astype(BF16)
    picked = jnp.dot(select, grads_ref[...], preferred_element_type=F32)
    out_grads_ref[...] = (picked * scale_column).astype(BF16)


def route(ids, weight, rows, grads, slots, most):
    width = rows.shape[1]
    shape = jax.ShapeDtypeStruct((slots, width), BF16)
    return pl.pallas_call(
        functools.partial(route_kernel, most=most),
        out_shape=(shape, shape),
        name="route",
    )(ids, weight, rows, grads)


def home_kernel(ids_ref, weight_ref, back_ref, out_ref, *, most, weighted):
    ids = ids_ref[...]
    top, rows = ids.shape
    slots = back_ref.shape[0]
    experts = slots // most
    names, named, rank = ranks(ids, experts)
    want = lax.broadcasted_iota(jnp.int32, (experts, most, rows), 1).astype(F32)
    back = back_ref[...]
    columns = jnp.transpose(weight_ref[...]) if weighted else None
    total = None
    for k in range(top):
        place = jnp.where(names == ids[k : k + 1, :], rank, -1.0)
        select = jnp.where(want == place[:, None, :], 1.0, 0.0).reshape(slots, rows).astype(BF16)
        part = lax.dot_general(select, back, (((0,), (0,)), ((), ())), preferred_element_type=F32)
        if weighted:
            part = part * columns[:, k : k + 1]
        total = part if total is None else total + part
    out_ref[...] = total.astype(BF16)


def home(ids, weight, back, most, weighted):
    return pl.pallas_call(
        functools.partial(home_kernel, most=most, weighted=weighted),
        out_shape=jax.ShapeDtypeStruct((ids.shape[1], back.shape[1]), BF16),
        name="home",
    )(ids, weight, back)


def across(rows):
    experts = lax.axis_size("expert")
    slots, width = rows.shape
    return lax.all_to_all(
        rows.reshape(experts, slots // experts, width), "expert", split_axis=0, concat_axis=0, tiled=True
    ).reshape(slots, width)


def whole_rows(half):
    parts_count = lax.axis_size("mp")
    width = half.shape[1]
    parts = [half]
    for k in range(1, parts_count):
        parts.append(
            lax.ppermute(half, "mp", [((j + k) % parts_count, j) for j in range(parts_count)])
        )
    both = jnp.concatenate(parts + parts[:-1], axis=1)
    first = (parts_count - lax.axis_index("mp")) % parts_count
    return lax.dynamic_slice_in_dim(both, first * width, parts_count * width, axis=1)


def share(partial):
    parts_count = lax.axis_size("mp")
    me = lax.axis_index("mp")
    width = partial.shape[1] // parts_count
    partial = partial.astype(BF16)
    total = lax.dynamic_slice_in_dim(partial, me * width, width, axis=1).astype(F32)
    for k in range(1, parts_count):
        other = lax.dynamic_slice_in_dim(partial, ((me + k) % parts_count) * width, width, axis=1)
        got = lax.ppermute(other, "mp", [(j, (j + k) % parts_count) for j in range(parts_count)])
        total = total + got.astype(F32)
    return total.astype(BF16)


def shards(tokens, expert_ids, combine, w_gate, w_up, w_down, grad_out):
    row_count = tokens.shape[0]
    expert_count = lax.axis_size("expert")
    most = 4 * row_count // expert_count
    slots = expert_count * most
    w_gate, w_up, w_down = w_gate[0], w_up[0], w_down[0]
    ids, weight = expert_ids.T, combine.T
    row_slots, grad_slots = route(ids, weight, tokens, grad_out, slots, most)
    rows = across(row_slots)
    rows, grad_slots = lax.optimization_barrier((rows, grad_slots))
    grads = across(grad_slots)
    rows = whole_rows(rows)
    gate = jnp.dot(rows, w_gate, preferred_element_type=F32)
    up = jnp.dot(rows, w_up, preferred_element_type=F32)
    sig = jax.nn.sigmoid(gate)
    hidden = (gate * sig * up).astype(BF16)
    out_partial = jnp.dot(hidden, w_down, preferred_element_type=F32)
    out_share = share(out_partial)
    out_back = across(out_share)
    output = home(ids, weight, out_back, most, True)
    grads = whole_rows(grads)
    grad_hidden = lax.dot_general(grads, w_down, (((1,), (1,)), ((), ())), preferred_element_type=F32)
    down_grad = lax.dot_general(hidden, grads, (((0,), (0,)), ((), ())), preferred_element_type=F32)
    grad_up = (grad_hidden * gate * sig).astype(BF16)
    grad_gate = (grad_hidden * up * sig * (1.0 + gate * (1.0 - sig))).astype(BF16)
    terms = lax.dot_general(grad_gate, w_gate, (((1,), (1,)), ((), ())), preferred_element_type=F32)
    terms = terms + lax.dot_general(grad_up, w_up, (((1,), (1,)), ((), ())), preferred_element_type=F32)
    grad_back = across(share(terms))
    grad_tokens = home(ids, weight, grad_back, most, False)
    return output, grad_tokens, down_grad.astype(BF16)[None]


def solution(mesh):
    return jax.shard_map(
        shards,
        mesh=mesh,
        in_specs=(
            P("expert", "mp"),
            P("expert", None),
            P("expert", None),
            P("expert", None, "mp"),
            P("expert", None, "mp"),
            P("expert", "mp", None),
            P("expert", "mp"),
        ),
        out_specs=(P("expert", "mp"), P("expert", "mp"), P("expert", "mp", None)),
        check_vma=False,
    )
```

```python
import functools

import jax
import jax.numpy as jnp
from jax import lax
from jax.experimental import pallas as pl
from jax.experimental.pallas import tpu as pltpu
from jax.sharding import PartitionSpec as P


F32 = jnp.float32
BF16 = jnp.bfloat16
SMEM = pl.BlockSpec(memory_space=pltpu.SMEM)
VMEM = pl.BlockSpec(memory_space=pltpu.VMEM)


def cost(flops, nbytes):
    return pl.CostEstimate(flops=flops, bytes_accessed=nbytes, transcendentals=0)


def ranks(ids, first, experts):
    top, rows = ids.shape
    names = lax.broadcasted_iota(jnp.int32, (experts, rows), 0) + first
    named = names == ids[0:1, :]
    for k in range(1, top):
        named = named | (names == ids[k : k + 1, :])
    before = lax.broadcasted_iota(jnp.int32, (rows, rows), 0) < lax.broadcasted_iota(
        jnp.int32, (rows, rows), 1
    )
    rank = jnp.dot(
        jnp.where(named, 1.0, 0.0).astype(BF16),
        jnp.where(before, 1.0, 0.0).astype(BF16),
        preferred_element_type=F32,
    )
    return names, named, rank


def split_table(refs, top):
    if len(refs) == 2:
        return refs[0][...], refs[1][...]
    table = refs[0][...]
    return table[:top, :].astype(jnp.int32), table[top:, :]


def take(refs, counts):
    groups, at = [], 0
    for count in counts:
        groups.append(refs[at : at + count])
        at += count
    return groups, refs[at:]


def slots_kernel(first_ref, *refs, counts, most, top, scaled):
    groups, rest = take(refs, counts)
    out_ref = rest[-1]
    experts = out_ref.shape[0]
    first = first_ref[0]
    for s, group in enumerate(groups):
        ids, weight = split_table(group, top)
        rows = rest[s][...]
        count = rows.shape[0]
        names, named, rank = ranks(ids, first, experts)
        place = jnp.where(named, rank, -1.0)
        want = lax.broadcasted_iota(jnp.int32, (experts, most, count), 1).astype(F32)
        hit = want == place[:, None, :]
        select = jnp.where(hit, 1.0, 0.0).reshape(experts * most, count).astype(BF16)
        picked = jnp.dot(select, rows, preferred_element_type=F32)
        if scaled:
            scale = jnp.zeros((experts, count), F32)
            for k in range(top):
                scale = scale + jnp.where(names == ids[k : k + 1, :], weight[k : k + 1, :], 0.0)
            spread = jnp.where(hit, jnp.broadcast_to(scale[:, None, :], hit.shape), 0.0)
            picked = picked * jnp.sum(spread.reshape(experts * most, count), axis=1, keepdims=True)
        out_ref[:, s * most : (s + 1) * most, :] = picked.astype(BF16).reshape(experts, most, -1)


def build_slots(first, tables, rows, experts, most, top, scaled):
    flat = [t for table in tables for t in table]
    count, width = rows[0].shape
    return pl.pallas_call(
        functools.partial(
            slots_kernel, counts=[len(t) for t in tables], most=most, top=top, scaled=scaled
        ),
        in_specs=[SMEM] + [VMEM] * (len(flat) + len(rows)),
        out_specs=VMEM,
        out_shape=jax.ShapeDtypeStruct((experts, len(rows) * most, width), BF16),
        cost_estimate=cost(
            2 * len(rows) * experts * most * count * width, 2 * len(rows) * (count + experts * most) * width
        ),
        name="slots",
    )(first, *flat, *rows)


def home_kernel(first_ref, *refs, counts, at, most, top, weighted):
    groups, rest = take(refs, counts)
    back_ref = rest[0]
    outs = rest[1:]
    experts, _, width = back_ref.shape
    first = first_ref[0]
    for s, group in enumerate(groups):
        ids, weight = split_table(group, top)
        count = ids.shape[1]
        names, named, rank = ranks(ids, first, experts)
        want = lax.broadcasted_iota(jnp.int32, (experts, most, count), 1).astype(F32)
        back = back_ref[:, at[s] * most : (at[s] + 1) * most, :].reshape(experts * most, width)
        picks = [names == ids[k : k + 1, :] for k in range(top)] if weighted else [named]
        columns = jnp.transpose(weight) if weighted else None
        total = None
        for k, chosen in enumerate(picks):
            place = jnp.where(chosen, rank, -1.0)
            select = jnp.where(want == place[:, None, :], 1.0, 0.0)
            select = select.reshape(experts * most, count).astype(BF16)
            part = lax.dot_general(select, back, (((0,), (0,)), ((), ())), preferred_element_type=F32)
            if weighted:
                part = part * columns[:, k : k + 1]
            total = part if total is None else total + part
        outs[s][...] = total.astype(outs[s].dtype)


def bring_home(first, tables, back, at, kinds, count, most, top, weighted):
    flat = [t for table in tables for t in table]
    width = back.shape[2]
    return pl.pallas_call(
        functools.partial(
            home_kernel, counts=[len(t) for t in tables], at=at, most=most, top=top, weighted=weighted
        ),
        in_specs=[SMEM] + [VMEM] * (len(flat) + 1),
        out_specs=[VMEM] * len(tables),
        out_shape=[jax.ShapeDtypeStruct((count, width), kind) for kind in kinds],
        cost_estimate=cost(2 * back.size * count * (top if weighted else 1), 2 * back.size),
        name="home",
    )(first, *flat, back)


def blocks(hidden_width):
    return 256 if hidden_width % 256 == 0 else hidden_width


def spans(me_ref, parts, width):
    return [pl.ds(pl.multiple_of(lax.rem(me_ref[0] + k, parts) * width, width), width) for k in range(parts)]


NT = (((1,), (1,)), ((), ()))
TN = (((0,), (0,)), ((), ()))


def weight_kernel(me_ref, *refs, parts, width, chunks):
    gs, hiddens, out_ref = refs[:parts], refs[parts:-1], refs[-1]
    where = spans(me_ref, parts, width)
    experts, _, most, _ = gs[0].shape
    for k in range(parts):
        g = gs[k][...].reshape(experts * chunks * most, width)
        total = lax.dot_general(hiddens[0][...], g, TN, preferred_element_type=F32)
        out_ref[0, :, where[k]] = total.astype(BF16)


def weight_grad(me, gs, hiddens):
    parts, (experts, chunks, most, width) = len(gs), gs[0].shape
    rows, hid = hiddens[0].shape
    block = blocks(hid)
    whole = pl.BlockSpec((experts, chunks, most, width), lambda j: (0, 0, 0, 0))
    return pl.pallas_call(
        functools.partial(weight_kernel, parts=parts, width=width, chunks=chunks),
        grid=(hid // block,),
        in_specs=[SMEM] + [whole] * parts + [pl.BlockSpec((rows, block), lambda j: (0, j))],
        out_specs=pl.BlockSpec((1, block, parts * width), lambda j: (0, j, 0)),
        out_shape=jax.ShapeDtypeStruct((1, hid, parts * width), BF16),
        cost_estimate=cost(2 * chunks * rows * hid * parts * width, 2 * hid * parts * width),
        name="weight_grad",
    )(me, *gs, *hiddens)


def over(value):
    experts = lax.axis_size("expert")
    return lax.ppermute(value, "expert", [(j, (j + experts // 2) % experts) for j in range(experts)])


def within(slots):
    experts = lax.axis_size("expert")
    groups = [list(range(experts // 2)), list(range(experts // 2, experts))]
    return lax.all_to_all(
        slots, "expert", split_axis=0, concat_axis=0, tiled=True, axis_index_groups=groups
    )


def gather_parts(value):
    parts = lax.axis_size("mp")
    return [value] + [lax.ppermute(value, "mp", [((j + k) % parts, j) for j in range(parts)]) for k in range(1, parts)]


def give_parts(values):
    parts = lax.axis_size("mp")
    return [values[0]] + [
        lax.ppermute(values[k], "mp", [(j, (j + k) % parts) for j in range(parts)])
        for k in range(1, parts)
    ]


def added(values):
    total = values[0].astype(F32)
    for value in values[1:]:
        total = total + value.astype(F32)
    return total.astype(BF16)


def rank_slices(weight, axis):
    parts = lax.axis_size("mp")
    width = weight.shape[axis] // parts
    me = lax.axis_index("mp")
    return [
        lax.dynamic_slice_in_dim(weight, ((me + k) % parts) * width, width, axis=axis) for k in range(parts)
    ]


def dot(a, b, dims=(((1,), (0,)), ((), ()))):
    return lax.dot_general(a, b, dims, preferred_element_type=F32)


def joined(parts):
    count, width = len(parts), parts[0].shape[1]
    both = jnp.concatenate(parts + parts[:-1], axis=1)
    first = (count - lax.axis_index("mp")) % count
    return lax.dynamic_slice_in_dim(both, first * width, count * width, axis=1)


def body(tokens, expert_ids, combine, w_gate, w_up, w_down, grad_out):
    row_count, top = expert_ids.shape
    expert_count = lax.axis_size("expert")
    most = 4 * row_count // expert_count
    half = expert_count // 2
    width = tokens.shape[1]
    rows = 2 * half * most
    gates, ups, downs = rank_slices(w_gate[0], 0), rank_slices(w_up[0], 0), rank_slices(w_down[0], 1)
    first = ((lax.axis_index("expert") // half) * half).astype(jnp.int32).reshape(1)
    me = lax.axis_index("mp").astype(jnp.int32).reshape(1)
    near = (expert_ids.T, combine.T)
    far_tokens = over(tokens)
    far = (over(jnp.concatenate([near[0].astype(F32), near[1]], axis=0)),)
    far_grads = over(grad_out)
    t_slots = build_slots(first, (near, far), (tokens, far_tokens), half, most, top, False)
    t_rows = within(t_slots)
    grad_slots = build_slots(first, (near, far), (grad_out, far_grads), half, most, top, True)
    grads = within(grad_slots)
    xs = gather_parts(t_rows.reshape(rows, width))
    x = joined(xs)
    gate = dot(x, w_gate[0])
    up = dot(x, w_up[0])
    sig = jax.nn.sigmoid(gate)
    hidden = (gate * sig * up).astype(BF16)
    outs = [dot(hidden, w).astype(BF16) for w in reversed(downs)][::-1]
    outs[0] = lax.optimization_barrier(outs[0])
    out_given = give_parts(outs)
    out_slots = added(out_given)
    grads, out_slots = lax.optimization_barrier((grads, out_slots))
    out_back = within(out_slots.reshape(half, 2 * most, width))
    out_near, out_far = bring_home(
        first, (near, far), out_back, (0, 1), (F32, BF16), row_count, most, top, True
    )
    out_over = over(out_far)
    output = (out_near + out_over.astype(F32)).astype(BF16)
    gs = gather_parts(grads.reshape(rows, width))
    g = joined(gs)
    grad_hidden = dot(g, w_down[0], NT)
    grad_up = (grad_hidden * gate * sig).astype(BF16)
    grad_gate = (grad_hidden * up * sig * (1.0 + gate * (1.0 - sig))).astype(BF16)
    terms = []
    for k in reversed(range(len(gs))):
        terms.append((dot(grad_gate, gates[k], NT) + dot(grad_up, ups[k], NT)).astype(BF16))
    terms = terms[::-1]
    terms[0] = lax.optimization_barrier(terms[0])
    given = give_parts(terms)
    down_grad = weight_grad(me, [g.reshape(half, 2, most, width) for g in gs], (hidden,))
    grad_back = within(added(given).reshape(half, 2 * most, width))
    grad_near, grad_far = bring_home(first, (near, far), grad_back, (0, 1), (F32, BF16), row_count, most, top, False)
    grad_over = over(grad_far)
    grad_tokens = (grad_near + grad_over.astype(F32)).astype(BF16)
    return output, grad_tokens, down_grad


def solution(mesh):
    return jax.shard_map(
        body,
        mesh=mesh,
        in_specs=(
            P("expert", "mp"),
            P("expert", None),
            P("expert", None),
            P("expert", None, "mp"),
            P("expert", None, "mp"),
            P("expert", "mp", None),
            P("expert", "mp"),
        ),
        out_specs=(P("expert", "mp"), P("expert", "mp"), P("expert", "mp", None)),
        check_vma=False,
    )
```

```python
import functools

import jax
import jax.numpy as jnp
from jax import lax
from jax.experimental import pallas as pl
from jax.experimental.pallas import tpu as pltpu
from jax.sharding import PartitionSpec as P


F32 = jnp.float32
BF16 = jnp.bfloat16
SMEM = pl.BlockSpec(memory_space=pltpu.SMEM)
VMEM = pl.BlockSpec(memory_space=pltpu.VMEM)


def cost(flops, nbytes):
    return pl.CostEstimate(flops=flops, bytes_accessed=nbytes, transcendentals=0)


def ranks(ids, first, experts):
    top, rows = ids.shape
    names = lax.broadcasted_iota(jnp.int32, (experts, rows), 0) + first
    named = names == ids[0:1, :]
    for k in range(1, top):
        named = named | (names == ids[k : k + 1, :])
    before = lax.broadcasted_iota(jnp.int32, (rows, rows), 0) < lax.broadcasted_iota(
        jnp.int32, (rows, rows), 1
    )
    rank = jnp.dot(
        jnp.where(named, 1.0, 0.0).astype(BF16),
        jnp.where(before, 1.0, 0.0).astype(BF16),
        preferred_element_type=F32,
    )
    return names, named, rank


def split_table(refs, top):
    if len(refs) == 2:
        return refs[0][...], refs[1][...]
    table = refs[0][...]
    return table[:top, :].astype(jnp.int32), table[top:, :]


def take(refs, counts):
    groups, at = [], 0
    for count in counts:
        groups.append(refs[at : at + count])
        at += count
    return groups, refs[at:]


def slots_kernel(first_ref, *refs, counts, most, top, scaled):
    groups, rest = take(refs, counts)
    out_ref = rest[-1]
    experts = out_ref.shape[0]
    first = first_ref[0]
    for s, group in enumerate(groups):
        ids, weight = split_table(group, top)
        rows = rest[s][...]
        count = rows.shape[0]
        names, named, rank = ranks(ids, first, experts)
        place = jnp.where(named, rank, -1.0)
        want = lax.broadcasted_iota(jnp.int32, (experts, most, count), 1).astype(F32)
        hit = want == place[:, None, :]
        select = jnp.where(hit, 1.0, 0.0).reshape(experts * most, count).astype(BF16)
        picked = jnp.dot(select, rows, preferred_element_type=F32)
        if scaled:
            scale = jnp.zeros((experts, count), F32)
            for k in range(top):
                scale = scale + jnp.where(names == ids[k : k + 1, :], weight[k : k + 1, :], 0.0)
            spread = jnp.where(hit, jnp.broadcast_to(scale[:, None, :], hit.shape), 0.0)
            picked = picked * jnp.sum(spread.reshape(experts * most, count), axis=1, keepdims=True)
        out_ref[:, s * most : (s + 1) * most, :] = picked.astype(BF16).reshape(experts, most, -1)


def build_slots(first, tables, rows, experts, most, top, scaled):
    flat = [t for table in tables for t in table]
    count, width = rows[0].shape
    return pl.pallas_call(
        functools.partial(
            slots_kernel, counts=[len(t) for t in tables], most=most, top=top, scaled=scaled
        ),
        in_specs=[SMEM] + [VMEM] * (len(flat) + len(rows)),
        out_specs=VMEM,
        out_shape=jax.ShapeDtypeStruct((experts, len(rows) * most, width), BF16),
        cost_estimate=cost(
            2 * len(rows) * experts * most * count * width, 2 * len(rows) * (count + experts * most) * width
        ),
        name="slots",
    )(first, *flat, *rows)


def home_kernel(first_ref, *refs, counts, at, most, top, weighted):
    groups, rest = take(refs, counts)
    back_ref = rest[0]
    outs = rest[1:]
    experts, _, width = back_ref.shape
    first = first_ref[0]
    for s, group in enumerate(groups):
        ids, weight = split_table(group, top)
        count = ids.shape[1]
        names, named, rank = ranks(ids, first, experts)
        want = lax.broadcasted_iota(jnp.int32, (experts, most, count), 1).astype(F32)
        back = back_ref[:, at[s] * most : (at[s] + 1) * most, :].reshape(experts * most, width)
        picks = [names == ids[k : k + 1, :] for k in range(top)] if weighted else [named]
        columns = jnp.transpose(weight) if weighted else None
        total = None
        for k, chosen in enumerate(picks):
            place = jnp.where(chosen, rank, -1.0)
            select = jnp.where(want == place[:, None, :], 1.0, 0.0)
            select = select.reshape(experts * most, count).astype(BF16)
            part = lax.dot_general(select, back, (((0,), (0,)), ((), ())), preferred_element_type=F32)
            if weighted:
                part = part * columns[:, k : k + 1]
            total = part if total is None else total + part
        outs[s][...] = total.astype(outs[s].dtype)


def bring_home(first, tables, back, at, kinds, count, most, top, weighted):
    flat = [t for table in tables for t in table]
    width = back.shape[2]
    return pl.pallas_call(
        functools.partial(
            home_kernel, counts=[len(t) for t in tables], at=at, most=most, top=top, weighted=weighted
        ),
        in_specs=[SMEM] + [VMEM] * (len(flat) + 1),
        out_specs=[VMEM] * len(tables),
        out_shape=[jax.ShapeDtypeStruct((count, width), kind) for kind in kinds],
        cost_estimate=cost(2 * back.size * count * (top if weighted else 1), 2 * back.size),
        name="home",
    )(first, *flat, back)


def blocks(hidden_width):
    return 256 if hidden_width % 256 == 0 else hidden_width


def spans(me_ref, parts, width):
    return [pl.ds(pl.multiple_of(lax.rem(me_ref[0] + k, parts) * width, width), width) for k in range(parts)]


NT = (((1,), (1,)), ((), ()))
TN = (((0,), (0,)), ((), ()))


def weight_kernel(me_ref, *refs, parts, width, chunks):
    gs, hiddens, out_ref = refs[:parts], refs[parts:-1], refs[-1]
    where = spans(me_ref, parts, width)
    experts, _, most, _ = gs[0].shape
    for k in range(parts):
        g = gs[k][...].reshape(experts * chunks * most, width)
        total = lax.dot_general(hiddens[0][...], g, TN, preferred_element_type=F32)
        out_ref[0, :, where[k]] = total.astype(BF16)


def weight_grad(me, gs, hiddens):
    parts, (experts, chunks, most, width) = len(gs), gs[0].shape
    rows, hid = hiddens[0].shape
    block = blocks(hid)
    whole = pl.BlockSpec((experts, chunks, most, width), lambda j: (0, 0, 0, 0))
    return pl.pallas_call(
        functools.partial(weight_kernel, parts=parts, width=width, chunks=chunks),
        grid=(hid // block,),
        in_specs=[SMEM] + [whole] * parts + [pl.BlockSpec((rows, block), lambda j: (0, j))],
        out_specs=pl.BlockSpec((1, block, parts * width), lambda j: (0, j, 0)),
        out_shape=jax.ShapeDtypeStruct((1, hid, parts * width), BF16),
        cost_estimate=cost(2 * chunks * rows * hid * parts * width, 2 * hid * parts * width),
        name="weight_grad",
    )(me, *gs, *hiddens)


def over(value):
    experts = lax.axis_size("expert")
    return lax.ppermute(value, "expert", [(j, (j + experts // 2) % experts) for j in range(experts)])


def within(slots):
    experts = lax.axis_size("expert")
    groups = [list(range(experts // 2)), list(range(experts // 2, experts))]
    return lax.all_to_all(
        slots, "expert", split_axis=0, concat_axis=0, tiled=True, axis_index_groups=groups
    )


def gather_parts(value):
    parts = lax.axis_size("mp")
    return [value] + [lax.ppermute(value, "mp", [((j + k) % parts, j) for j in range(parts)]) for k in range(1, parts)]


def give_parts(values):
    parts = lax.axis_size("mp")
    return [values[0]] + [
        lax.ppermute(values[k], "mp", [(j, (j + k) % parts) for j in range(parts)])
        for k in range(1, parts)
    ]


def added(values):
    total = values[0].astype(F32)
    for value in values[1:]:
        total = total + value.astype(F32)
    return total.astype(BF16)


def rank_slices(weight, axis):
    parts = lax.axis_size("mp")
    width = weight.shape[axis] // parts
    me = lax.axis_index("mp")
    return [
        lax.dynamic_slice_in_dim(weight, ((me + k) % parts) * width, width, axis=axis) for k in range(parts)
    ]


def dot(a, b, dims=(((1,), (0,)), ((), ()))):
    return lax.dot_general(a, b, dims, preferred_element_type=F32)


def joined(parts):
    count, width = len(parts), parts[0].shape[1]
    both = jnp.concatenate(parts + parts[:-1], axis=1)
    first = (count - lax.axis_index("mp")) % count
    return lax.dynamic_slice_in_dim(both, first * width, count * width, axis=1)


def body(tokens, expert_ids, combine, w_gate, w_up, w_down, grad_out):
    row_count, top = expert_ids.shape
    expert_count = lax.axis_size("expert")
    most = 4 * row_count // expert_count
    half = expert_count // 2
    width = tokens.shape[1]
    rows = 2 * half * most
    gates, ups, downs = rank_slices(w_gate[0], 0), rank_slices(w_up[0], 0), rank_slices(w_down[0], 1)
    first = ((lax.axis_index("expert") // half) * half).astype(jnp.int32).reshape(1)
    me = lax.axis_index("mp").astype(jnp.int32).reshape(1)
    near = (expert_ids.T, combine.T)
    far_tokens = over(tokens)
    near_slots = build_slots(first, (near,), (tokens,), half, most, top, False)
    far = (over(jnp.concatenate([near[0].astype(F32), near[1]], axis=0)),)
    near_rows = within(near_slots)
    far_grads = over(grad_out)
    far_slots = build_slots(first, (far,), (far_tokens,), half, most, top, False)
    far_rows = within(far_slots)
    grad_slots = build_slots(first, (near, far), (grad_out, far_grads), half, most, top, True)
    grads = within(grad_slots)
    near_parts = gather_parts(near_rows.reshape(rows // 2, width))
    far_parts = gather_parts(far_rows.reshape(rows // 2, width))
    xs = [
        jnp.concatenate([v.reshape(half, 1, most, width) for v in pair], axis=1).reshape(rows, width)
        for pair in zip(near_parts, far_parts)
    ]
    x = joined(xs)
    gate = dot(x, w_gate[0])
    up = dot(x, w_up[0])
    sig = jax.nn.sigmoid(gate)
    hidden = (gate * sig * up).astype(BF16)
    outs = [dot(hidden, w).astype(BF16) for w in reversed(downs)][::-1]
    outs[0] = lax.optimization_barrier(outs[0])
    out_given = give_parts(outs)
    out_slots = added(out_given)
    grads, out_slots = lax.optimization_barrier((grads, out_slots))
    out_back = within(out_slots.reshape(half, 2 * most, width))
    out_near, out_far = bring_home(
        first, (near, far), out_back, (0, 1), (F32, BF16), row_count, most, top, True
    )
    out_over = over(out_far)
    output = (out_near + out_over.astype(F32)).astype(BF16)
    gs = gather_parts(grads.reshape(rows, width))
    g = joined(gs)
    grad_hidden = dot(g, w_down[0], NT)
    grad_up = (grad_hidden * gate * sig).astype(BF16)
    grad_gate = (grad_hidden * up * sig * (1.0 + gate * (1.0 - sig))).astype(BF16)
    terms = []
    for k in reversed(range(len(gs))):
        terms.append((dot(grad_gate, gates[k], NT) + dot(grad_up, ups[k], NT)).astype(BF16))
    terms = terms[::-1]
    terms[0] = lax.optimization_barrier(terms[0])
    given = give_parts(terms)
    down_grad = weight_grad(me, [g.reshape(half, 2, most, width) for g in gs], (hidden,))
    grad_back = within(added(given).reshape(half, 2 * most, width))
    grad_near, grad_far = bring_home(first, (near, far), grad_back, (0, 1), (F32, BF16), row_count, most, top, False)
    grad_over = over(grad_far)
    grad_tokens = (grad_near + grad_over.astype(F32)).astype(BF16)
    return output, grad_tokens, down_grad


def solution(mesh):
    return jax.shard_map(
        body,
        mesh=mesh,
        in_specs=(
            P("expert", "mp"),
            P("expert", None),
            P("expert", None),
            P("expert", None, "mp"),
            P("expert", None, "mp"),
            P("expert", "mp", None),
            P("expert", "mp"),
        ),
        out_specs=(P("expert", "mp"), P("expert", "mp"), P("expert", "mp", None)),
        check_vma=False,
    )
```

```python
import functools

import jax
import jax.numpy as jnp
from jax import lax
from jax.experimental import pallas as pl
from jax.experimental.pallas import tpu as pltpu
from jax.sharding import PartitionSpec as P


F32 = jnp.float32
BF16 = jnp.bfloat16
SMEM = pl.BlockSpec(memory_space=pltpu.SMEM)
VMEM = pl.BlockSpec(memory_space=pltpu.VMEM)


def cost(flops, nbytes):
    return pl.CostEstimate(flops=flops, bytes_accessed=nbytes, transcendentals=0)


def ranks(ids, first, experts):
    top, rows = ids.shape
    names = lax.broadcasted_iota(jnp.int32, (experts, rows), 0) + first
    named = names == ids[0:1, :]
    for k in range(1, top):
        named = named | (names == ids[k : k + 1, :])
    before = lax.broadcasted_iota(jnp.int32, (rows, rows), 0) < lax.broadcasted_iota(
        jnp.int32, (rows, rows), 1
    )
    rank = jnp.dot(
        jnp.where(named, 1.0, 0.0).astype(BF16),
        jnp.where(before, 1.0, 0.0).astype(BF16),
        preferred_element_type=F32,
    )
    return names, named, rank


def split_table(refs, top):
    if len(refs) == 2:
        return refs[0][...], refs[1][...]
    table = refs[0][...]
    return table[:top, :].astype(jnp.int32), table[top:, :]


def take(refs, counts):
    groups, at = [], 0
    for count in counts:
        groups.append(refs[at : at + count])
        at += count
    return groups, refs[at:]


def slots_kernel(first_ref, *refs, counts, most, top, scaled):
    groups, rest = take(refs, counts)
    out_ref = rest[-1]
    experts = out_ref.shape[0]
    first = first_ref[0]
    for s, group in enumerate(groups):
        ids, weight = split_table(group, top)
        rows = rest[s][...]
        count = rows.shape[0]
        names, named, rank = ranks(ids, first, experts)
        place = jnp.where(named, rank, -1.0)
        want = lax.broadcasted_iota(jnp.int32, (experts, most, count), 1).astype(F32)
        hit = want == place[:, None, :]
        select = jnp.where(hit, 1.0, 0.0).reshape(experts * most, count).astype(BF16)
        picked = jnp.dot(select, rows, preferred_element_type=F32)
        if scaled:
            scale = jnp.zeros((experts, count), F32)
            for k in range(top):
                scale = scale + jnp.where(names == ids[k : k + 1, :], weight[k : k + 1, :], 0.0)
            spread = jnp.where(hit, jnp.broadcast_to(scale[:, None, :], hit.shape), 0.0)
            picked = picked * jnp.sum(spread.reshape(experts * most, count), axis=1, keepdims=True)
        out_ref[:, s * most : (s + 1) * most, :] = picked.astype(BF16).reshape(experts, most, -1)


def build_slots(first, tables, rows, experts, most, top, scaled):
    flat = [t for table in tables for t in table]
    count, width = rows[0].shape
    return pl.pallas_call(
        functools.partial(
            slots_kernel, counts=[len(t) for t in tables], most=most, top=top, scaled=scaled
        ),
        in_specs=[SMEM] + [VMEM] * (len(flat) + len(rows)),
        out_specs=VMEM,
        out_shape=jax.ShapeDtypeStruct((experts, len(rows) * most, width), BF16),
        cost_estimate=cost(
            2 * len(rows) * experts * most * count * width, 2 * len(rows) * (count + experts * most) * width
        ),
        name="slots",
    )(first, *flat, *rows)


def home_kernel(first_ref, *refs, counts, at, most, top, weighted):
    groups, rest = take(refs, counts)
    back_ref = rest[0]
    outs = rest[1:]
    experts, _, width = back_ref.shape
    first = first_ref[0]
    for s, group in enumerate(groups):
        ids, weight = split_table(group, top)
        count = ids.shape[1]
        names, named, rank = ranks(ids, first, experts)
        want = lax.broadcasted_iota(jnp.int32, (experts, most, count), 1).astype(F32)
        back = back_ref[:, at[s] * most : (at[s] + 1) * most, :].reshape(experts * most, width)
        picks = [names == ids[k : k + 1, :] for k in range(top)] if weighted else [named]
        columns = jnp.transpose(weight) if weighted else None
        total = None
        for k, chosen in enumerate(picks):
            place = jnp.where(chosen, rank, -1.0)
            select = jnp.where(want == place[:, None, :], 1.0, 0.0)
            select = select.reshape(experts * most, count).astype(BF16)
            part = lax.dot_general(select, back, (((0,), (0,)), ((), ())), preferred_element_type=F32)
            if weighted:
                part = part * columns[:, k : k + 1]
            total = part if total is None else total + part
        outs[s][...] = total.astype(outs[s].dtype)


def bring_home(first, tables, back, at, kinds, count, most, top, weighted):
    flat = [t for table in tables for t in table]
    width = back.shape[2]
    return pl.pallas_call(
        functools.partial(
            home_kernel, counts=[len(t) for t in tables], at=at, most=most, top=top, weighted=weighted
        ),
        in_specs=[SMEM] + [VMEM] * (len(flat) + 1),
        out_specs=[VMEM] * len(tables),
        out_shape=[jax.ShapeDtypeStruct((count, width), kind) for kind in kinds],
        cost_estimate=cost(2 * back.size * count * (top if weighted else 1), 2 * back.size),
        name="home",
    )(first, *flat, back)


def selectors_kernel(first_ref, *refs, counts, most, top):
    groups, outs = take(refs, counts)
    experts = outs[0].shape[0]
    first = first_ref[0]
    for s, group in enumerate(groups):
        ids, _ = split_table(group, top)
        count = ids.shape[1]
        _, named, rank = ranks(ids, first, experts)
        place = jnp.where(named, rank, -1.0)
        want = lax.broadcasted_iota(jnp.int32, (experts, most, count), 1).astype(F32)
        select = jnp.where(want == place[:, None, :], 1.0, 0.0).astype(BF16)
        for at in range(len(groups)):
            outs[s][:, at * most : (at + 1) * most, :] = select if at == s else jnp.zeros_like(select)


def selectors(first, tables, experts, most, count, top):
    flat = [t for table in tables for t in table]
    shape = jax.ShapeDtypeStruct((experts, len(tables) * most, count), BF16)
    result = pl.pallas_call(
        functools.partial(selectors_kernel, counts=[len(t) for t in tables], most=most, top=top),
        in_specs=[SMEM] + [VMEM] * len(flat),
        out_specs=[VMEM] * len(tables),
        out_shape=[shape] * len(tables),
        name="selectors",
    )(first, *flat)
    return [r.reshape(-1, count) for r in result]


def blocks(hidden_width):
    return 256 if hidden_width % 256 == 0 else hidden_width


def spans(me_ref, parts, width):
    return [pl.ds(pl.multiple_of(lax.rem(me_ref[0] + k, parts) * width, width), width) for k in range(parts)]


NT = (((1,), (1,)), ((), ()))
TN = (((0,), (0,)), ((), ()))


def weight_kernel(me_ref, *refs, parts, width, chunks):
    gs, hiddens, out_ref = refs[:parts], refs[parts:-1], refs[-1]
    where = spans(me_ref, parts, width)
    experts, _, most, _ = gs[0].shape
    for k in range(parts):
        g = gs[k][...].reshape(experts * chunks * most, width)
        total = lax.dot_general(hiddens[0][...], g, TN, preferred_element_type=F32)
        out_ref[0, :, where[k]] = total.astype(BF16)


def weight_grad(me, gs, hiddens):
    parts, (experts, chunks, most, width) = len(gs), gs[0].shape
    rows, hid = hiddens[0].shape
    block = blocks(hid)
    whole = pl.BlockSpec((experts, chunks, most, width), lambda j: (0, 0, 0, 0))
    return pl.pallas_call(
        functools.partial(weight_kernel, parts=parts, width=width, chunks=chunks),
        grid=(hid // block,),
        in_specs=[SMEM] + [whole] * parts + [pl.BlockSpec((rows, block), lambda j: (0, j))],
        out_specs=pl.BlockSpec((1, block, parts * width), lambda j: (0, j, 0)),
        out_shape=jax.ShapeDtypeStruct((1, hid, parts * width), BF16),
        cost_estimate=cost(2 * chunks * rows * hid * parts * width, 2 * hid * parts * width),
        name="weight_grad",
    )(me, *gs, *hiddens)


def over(value):
    experts = lax.axis_size("expert")
    flip = experts // 2 + (experts // 4 if experts & (experts - 1) == 0 else 0)
    pairs = [(j, j ^ flip if experts & (experts - 1) == 0 else (j + flip) % experts) for j in range(experts)]
    return lax.ppermute(value, "expert", pairs)


def within(slots):
    experts = lax.axis_size("expert")
    groups = [list(range(experts // 2)), list(range(experts // 2, experts))]
    return lax.all_to_all(
        slots, "expert", split_axis=0, concat_axis=0, tiled=True, axis_index_groups=groups
    )


def gather_parts(value):
    parts = lax.axis_size("mp")
    return [value] + [lax.ppermute(value, "mp", [((j + k) % parts, j) for j in range(parts)]) for k in range(1, parts)]


def give_parts(values):
    parts = lax.axis_size("mp")
    return [values[0]] + [
        lax.ppermute(values[k], "mp", [(j, (j + k) % parts) for j in range(parts)])
        for k in range(1, parts)
    ]


def added(values):
    total = values[0].astype(F32)
    for value in values[1:]:
        total = total + value.astype(F32)
    return total.astype(BF16)


def rank_slices(weight, axis):
    parts = lax.axis_size("mp")
    width = weight.shape[axis] // parts
    me = lax.axis_index("mp")
    return [
        lax.dynamic_slice_in_dim(weight, ((me + k) % parts) * width, width, axis=axis) for k in range(parts)
    ]


def in_vmem(value):
    return pltpu.with_memory_space_constraint(value, pltpu.VMEM)


def dot(a, b, dims=(((1,), (0,)), ((), ()))):
    return lax.dot_general(a, b, dims, preferred_element_type=F32)


def joined(parts):
    count, width = len(parts), parts[0].shape[1]
    both = jnp.concatenate(parts + parts[:-1], axis=1)
    first = (count - lax.axis_index("mp")) % count
    return lax.dynamic_slice_in_dim(both, first * width, count * width, axis=1)


def body(tokens, expert_ids, combine, w_gate, w_up, w_down, grad_out):
    row_count, top = expert_ids.shape
    expert_count = lax.axis_size("expert")
    most = 4 * row_count // expert_count
    half = expert_count // 2
    width = tokens.shape[1]
    rows = 2 * half * most
    gates, ups = rank_slices(w_gate[0], 0), rank_slices(w_up[0], 0)
    downs = list(lax.optimization_barrier(tuple(rank_slices(w_down[0], 1))))
    first = ((lax.axis_index("expert") // half) * half).astype(jnp.int32).reshape(1)
    me = lax.axis_index("mp").astype(jnp.int32).reshape(1)
    near = (expert_ids.T, combine.T)
    far_tokens = over(tokens)
    near_slots = build_slots(first, (near,), (tokens,), half, most, top, False)
    far = (over(jnp.concatenate([near[0].astype(F32), near[1]], axis=0)),)
    near_rows = within(near_slots)
    far_grads = over(grad_out)
    far_slots = build_slots(first, (far,), (in_vmem(far_tokens),), half, most, top, False)
    far_rows = within(far_slots)
    grad_slots = build_slots(first, (near, far), (grad_out, in_vmem(far_grads)), half, most, top, True)
    grads = within(grad_slots)
    near_parts = gather_parts(near_rows.reshape(rows // 2, width))
    far_parts = gather_parts(far_rows.reshape(rows // 2, width))
    xs = [
        jnp.concatenate([v.reshape(half, 1, most, width) for v in pair], axis=1).reshape(rows, width)
        for pair in zip(near_parts, far_parts)
    ]
    x = joined(xs)
    gate = dot(x, w_gate[0])
    up = dot(x, w_up[0])
    sig = jax.nn.sigmoid(gate)
    hidden = (gate * sig * up).astype(BF16)
    by_up = (gate * sig).astype(BF16)
    by_gate = (up * sig * (1.0 + gate * (1.0 - sig))).astype(BF16)
    hidden, by_up, by_gate = lax.optimization_barrier((hidden, by_up, by_gate))
    outs = [dot(hidden, w).astype(BF16) for w in reversed(downs)][::-1]
    outs[0] = lax.optimization_barrier(outs[0])
    out_given = give_parts(outs)
    out_slots = added(out_given)
    grads, out_slots = lax.optimization_barrier((grads, out_slots))
    out_back = within(out_slots.reshape(half, 2 * most, width))
    out_near, out_far = bring_home(
        first, (near, far), out_back, (0, 1), (F32, BF16), row_count, most, top, True
    )
    out_over = over(out_far)
    output = (out_near + out_over.astype(F32)).astype(BF16)
    gs = gather_parts(grads.reshape(rows, width))
    g = lax.optimization_barrier(joined(gs))
    grad_hidden = dot(g, w_down[0], NT)
    grad_up = (grad_hidden * by_up.astype(F32)).astype(BF16)
    grad_gate = (grad_hidden * by_gate.astype(F32)).astype(BF16)
    terms = []
    for k in reversed(range(len(gs))):
        terms.append((dot(grad_gate, gates[k], NT) + dot(grad_up, ups[k], NT)).astype(BF16))
    terms = terms[::-1]
    terms[0] = lax.optimization_barrier(terms[0])
    given = give_parts(terms)
    down_grad = weight_grad(me, [g.reshape(half, 2, most, width) for g in gs], (hidden,))
    grad_back = within(added(given).reshape(half, 2 * most, width))
    near_select, far_select = selectors(first, (near, far), half, most, row_count, top)
    grad_back = grad_back.reshape(rows, width)
    grad_far = dot(far_select, grad_back, TN).astype(BF16)
    grad_near = dot(near_select, grad_back, TN)
    grad_over = over(grad_far)
    grad_tokens = (grad_near + grad_over.astype(F32)).astype(BF16)
    return output, grad_tokens, down_grad


def solution(mesh):
    return jax.shard_map(
        body,
        mesh=mesh,
        in_specs=(
            P("expert", "mp"),
            P("expert", None),
            P("expert", None),
            P("expert", None, "mp"),
            P("expert", None, "mp"),
            P("expert", "mp", None),
            P("expert", "mp"),
        ),
        out_specs=(P("expert", "mp"), P("expert", "mp"), P("expert", "mp", None)),
        check_vma=False,
    )
```
